32 devices in a mesh: scheme: 8 (over z, y), scen: 4 (over x, core).
Axes of the slice: x: 2, y: 2, z: 4, core: 2. Of those that a mesh axis runs over, the one named last changes fastest.
Arguments:
- cashflow: bfloat16 [1024, 400], P('scheme'), may hold values from 0.00049972534 to 0.0099487305
- assets0: float32 [1024], P('scheme'), may hold values from 0.5 to 2
- alloc: int32 [1024, 3], P('scheme'), may hold values from 0 to 39
- share: float32 [1024, 3], P('scheme'), may hold values from 0.2 to 1
- owner: int32 [1024, 1], P('scheme'), may hold values from 0 to 7; in each aligned block of 128 rows (0 to 127, 128 to 255, ...) at most 32 rows name the same one
- flags: int32 [1024, 2, 1024], P('scheme', None, 'scen'), may hold values 0 or 1
- rates: float32 [2, 100, 1024], P(None, None, 'scen'), may hold values from 0.0035 to 0.07
- inflation: float32 [2, 100, 1024], P(None, None, 'scen'), may hold values from 0 to 0.056
- returns: float32 [2, 40, 1024], P(None, None, 'scen'), may hold values from -0.6 to 0.6
- basis: bfloat16 [8, 400, 1024], P('scheme', None, 'scen'), may hold values from 0.37 to 1.96
Outputs:
- book: float32 [8, 2, 1024], P('scheme', None, 'scen')
- levy: float32 [1024, 2, 1024], P('scheme', None, 'scen')
The draws below stay inside these ranges and needn't reach their ends.
Inputs may be any that keep to these rules, and one draw needn't show every extreme that they name: Among the 128 schemes of one device's aligned block, no book owner is named more than 32 times, a bound that some block reaches.
All inputs are finite; a program needn't handle non-finite values. No bound on the sum of `flags` on one device may be relied on, other than what follows from the above.
Results may differ from the reference program's by a relative error of at most 0.0005.
Values may be sent and summed in bfloat16 or wider, within the bound.
A program may use at most 64 MiB of HBM per device.

```python
import math
import jax
import jax.numpy as jnp
import numpy as np
from jax import lax

SCH_DEV = 128
YEARS = 2
TR = 4
HOR = 100
CLASSES = 40
HOLD = 3
SCHEMES = 1024
SCEN = 1024
OWNERS = 8
CAP = 32
N_SCHEME = 8


def scenario_levels(key):
    level_key = jax.random.fold_in(key, 11)
    frac_key = jax.random.fold_in(key, 12)
    level = jax.random.uniform(level_key, (YEARS, 1, SCEN), jnp.float32, 0.005, 0.05)
    fraction = jax.random.uniform(frac_key, (YEARS, 1, SCEN), jnp.float32, 0.0, 0.8)
    return (level, fraction)


def draw_rates(key, part):
    level, fraction = scenario_levels(key)
    rough = jax.random.uniform(jax.random.fold_in(key, 21), (YEARS, HOR, SCEN), jnp.float32, 0.7, 1.4)
    return level * rough


def draw_inflation(key, part):
    level, fraction = scenario_levels(key)
    rough = jax.random.uniform(jax.random.fold_in(key, 22), (YEARS, HOR, SCEN), jnp.float32, 0.7, 1.4)
    return level * fraction * rough


def draw_basis(key, part):
    level_key = jax.random.fold_in(key, 31)
    rough_key = jax.random.fold_in(key, 32)
    level = jax.random.uniform(level_key, (OWNERS, 1, SCEN), jnp.float32, 0.5, 1.5)
    rough = jax.random.uniform(rough_key, (OWNERS, TR * HOR, SCEN), jnp.float32, 0.75, 1.3)
    return (level * rough).astype(jnp.bfloat16)


def plant(result, key, least, high):
    spot = [jax.random.randint(jax.random.fold_in(key, axis), (), 0, length) for axis, length in enumerate(result.shape)]
    longest = result.shape.index(max(result.shape))
    neighbour = spot[:longest] + [(spot[longest] + 1) % result.shape[longest]] + spot[longest + 1:]
    return result.at[tuple(spot)].set(least).at[tuple(neighbour)].set(high)


def block_levels(own_key, dims, shards, low, largest):
    def one(position, parts):
        steps = jax.random.uniform(jax.random.fold_in(jax.random.fold_in(own_key, 6), position), (parts,), jnp.float32, low / len(shards), largest / len(shards))
        return jnp.repeat(jnp.exp(steps), dims[position] // parts).reshape((-1,) + (1,) * (len(dims) - position - 1))

    level = one(*shards[0])
    for cut in shards[1:]:
        level = level * one(*cut)
    return level


def shared_out(rng, own, number, rows, number_of, top, bound, lean):
    order = jax.random.permutation(rng, number_of)
    heavy_load, ordinary = load_shares(number_of, rows * top, bound, lean, True), load_shares(number_of, rows * top, bound, lean, False)
    places = jnp.arange(number_of)

    def named(lengths, turn):
        used = int((lengths > 0).sum())
        fixed = max(1, used // 4)
        shifted = fixed + (places - fixed + turn * (used - fixed)) % max(1, number_of - fixed)
        return jnp.zeros((number_of,), jnp.int32).at[order[jnp.where(places < fixed, places, shifted)]].set(jnp.asarray(lengths, jnp.int32))

    lengths = jnp.where(number % 4 == 0, named(heavy_load, number // 4), named(ordinary, number - number // 4 - 1))
    mixed = jax.random.permutation(jax.random.fold_in(own, 3), number_of)
    donor, receiver = mixed[0:number_of // 2 * 2:2], mixed[1:number_of // 2 * 2:2]
    room = jnp.minimum(lengths[donor] - 1, bound - lengths[receiver]) // 2
    room = jnp.where((donor == order[0]) | (receiver == order[0]) | (lengths[receiver] == 0), 0, jnp.maximum(room, 0))
    shifted = jax.random.randint(jax.random.fold_in(own, 4), (number_of // 2,), 0, 1 << 20) % (room + 1)
    lengths = lengths.at[donor].add(-shifted).at[receiver].add(shifted)
    members = jnp.searchsorted(jnp.cumsum(lengths), jnp.arange(rows * top), side="right").astype(jnp.int32)
    listing = members.reshape(top, rows).T
    listing = listing[jax.random.permutation(jax.random.fold_in(own, 1), rows)]
    turn = jax.random.randint(jax.random.fold_in(own, 2), (rows, 1), 0, top)
    return jnp.take_along_axis(listing, (jnp.arange(top)[None, :] + turn) % top, axis=1)


def load_shares(number_of, total, bound, lean, full):
    portions = [(1 << 20) // math.isqrt(grade ** lean) + 1 for grade in range(1, number_of + 1)]
    largest = bound if full else min(bound, max(-(-total // number_of), total * portions[0] // sum(portions)))
    least = 1 if total - largest >= number_of - 1 else 0
    holding, surplus = [largest] + [least] * (number_of - 1), total - largest - least * (number_of - 1)
    while surplus > 0:
        candidates = [i for i in range(1, number_of) if holding[i] < largest] or [i for i in range(1, number_of) if holding[i] < bound]
        whole, left = sum([portions[i] for i in candidates]), surplus
        for i in candidates:
            more = min(bound - holding[i], max(1, left * portions[i] // whole), surplus)
            holding[i] = holding[i] + more
            surplus = surplus - more
    return np.array(holding)


def bell_draw(key, dims, spread, bound, cuts=(), kind=jnp.bfloat16):
    factor_of = block_levels(key, dims, cuts, -0.22, 0.18) if cuts else 1.0
    values = jax.random.normal(key, dims, jnp.float32) * spread * factor_of
    return jnp.minimum(jnp.maximum(values, -bound), bound).astype(kind)


def setup_inputs(seed: int = 0) -> dict:
    keys = jax.random.split(jax.random.key(seed), 11)
    cashflow = jnp.clip(jnp.exp(math.log(0.0099487305) - 2.9911416 * jax.random.uniform(keys[0], (SCHEMES, TR * HOR), jnp.float32) ** block_levels(keys[0], (SCHEMES, TR * HOR), ((0, 8),), -0.2, 0.2)), 0.00049972534, 0.0099487305).astype(jnp.bfloat16)
    assets0 = jnp.clip(jnp.exp(math.log(2.0) - 1.3862944 * jax.random.uniform(keys[1], (SCHEMES,), jnp.float32) ** block_levels(keys[1], (SCHEMES,), ((0, 8),), -0.2, 0.2)), 0.5, 2.0)
    alloc = plant(jax.random.randint(keys[2], (SCHEMES, HOLD), 0, CLASSES), jax.random.fold_in(keys[2], 1), 0, CLASSES - 1).astype(jnp.int32)
    share = jnp.clip(0.2 + 0.8 * jax.random.uniform(keys[3], (SCHEMES, HOLD), jnp.float32) ** block_levels(keys[3], (SCHEMES, HOLD), ((0, 8),), -0.2, 0.2), 0.2, 1.0)
    owner_keys = jax.random.split(jax.random.fold_in(keys[4], 1), SCHEMES // SCH_DEV)
    owner_turns = jax.random.permutation(jax.random.fold_in(keys[4], 3), SCHEMES // SCH_DEV)
    owner = jax.vmap(lambda own, number: shared_out(jax.random.fold_in(keys[4], 2), own, number, SCH_DEV, N_SCHEME, 1, CAP, 2))(owner_keys, owner_turns).reshape((SCHEMES, 1))
    flags = plant((jax.random.randint(keys[5], (SCHEMES, YEARS, SCEN), 0, 4) < 1).astype(jnp.int32), jax.random.fold_in(keys[5], 1), 0, 1)
    rates = draw_rates(jax.random.fold_in(keys[10], 71), 0)
    inflation = draw_inflation(jax.random.fold_in(keys[10], 71), 0)
    returns = bell_draw(keys[8], (YEARS, CLASSES, SCEN), 0.15, 0.6, ((2, 4),), jnp.float32)
    basis = draw_basis(jax.random.fold_in(keys[10], 71), 0)
    return dict(cashflow=cashflow, assets0=assets0, alloc=alloc, share=share, owner=owner, flags=flags, rates=rates, inflation=inflation, returns=returns, basis=basis)


TRANCHE_INDEX = (0.0, 0.5, 1.0, 0.75)
COMP_LIMIT = 0.004


def discount(rate_year, infl_year):
    terms = (jnp.arange(HOR) + 1).astype(jnp.float32)[None, :, None]
    index = jnp.asarray(TRANCHE_INDEX, jnp.float32)[:, None, None]
    power = -terms * (rate_year[None] - index * infl_year[None])
    return jnp.exp(power).reshape(TR * HOR, rate_year.shape[1]).astype(jnp.bfloat16)


def exposures(alloc, share, classes):
    picks = (alloc[:, :, None] == jnp.arange(classes, dtype=jnp.int32)[None, None, :]).astype(jnp.float32)
    return jnp.sum(picks * share[:, :, None], axis=1)


def reference(cashflow, assets0, alloc, share, owner, flags, rates, inflation, returns, basis):
    exposure = exposures(alloc, share, CLASSES)
    comp = jnp.minimum(0.9 * cashflow.astype(jnp.float32), COMP_LIMIT).astype(jnp.bfloat16)
    assets = jnp.broadcast_to(assets0[:, None], (SCHEMES, SCEN))
    base = jnp.zeros((SCHEMES,), jnp.float32)
    discs = []
    held = []
    for year in range(YEARS):
        disc = discount(rates[year], inflation[year])
        liab = jnp.dot(cashflow, disc, preferred_element_type=jnp.float32)
        growth = jnp.dot(exposure, returns[year], precision=lax.Precision.HIGHEST)
        assets = assets * jnp.exp(growth)
        base = base + jnp.sum(jnp.maximum(liab - assets, 0.0) + 0.05 * liab, axis=1)
        discs.append(disc)
        held.append(assets)
    base = base / (SCEN * YEARS)
    held_all = jnp.stack(held, axis=1)
    owners_of = owner[:, 0]
    counts = jnp.sum((owners_of[:, None] == jnp.arange(OWNERS, dtype=jnp.int32)[None, :]).astype(jnp.int32), axis=0)
    starts = (jnp.cumsum(counts) - counts).astype(jnp.int32)
    most_owned = N_SCHEME * CAP
    order = jnp.argsort(owners_of, stable=True).astype(jnp.int32)
    padded = jnp.concatenate([order, jnp.zeros((most_owned,), jnp.int32)])

    def one_book(index):
        picked = lax.dynamic_slice_in_dim(padded, starts[index], most_owned)
        live = (jnp.arange(most_owned) < counts[index]).astype(jnp.float32)
        rows = comp[picked]
        totals = []
        for year in range(YEARS):
            factors = (basis[index].astype(jnp.float32) * discs[year].astype(jnp.float32)).astype(jnp.bfloat16)
            value = jnp.dot(rows, factors, preferred_element_type=jnp.float32)
            weight = flags[picked, year].astype(jnp.float32) * live[:, None]
            totals.append(jnp.sum(weight * (value - held_all[picked, year]), axis=0))
        return jnp.stack(totals)

    book = lax.map(one_book, jnp.arange(OWNERS, dtype=jnp.int32))
    claims = jnp.sum(book, axis=0)
    base_total = jnp.sum(base)
    levy = (claims / OWNERS)[None] * base[:, None, None] / (base_total / SCHEMES)
    return book, levy
```

```python
import functools

import jax
import jax.numpy as jnp
from jax import lax
from jax.experimental import pallas as pl
from jax.experimental.pallas import tpu as pltpu
from jax.sharding import PartitionSpec as P

TRANCHE_INDEX = (0.0, 0.5, 1.0, 0.75)
COMP_LIMIT = 0.004
HIGHEST = lax.Precision.HIGHEST
NT = (((1,), (1,)), ((), ()))
TN = (((0,), (0,)), ((), ()))


def each(low, high, body):
    if high - low <= 16:
        for i in range(low, high):
            body(i)
    else:
        lax.fori_loop(low, high, lambda i, c: (body(i), c)[1], 0)


def block(i, size):
    start = i * size
    return pl.ds(start if isinstance(start, int) else pl.multiple_of(start, size), size)


def kernel(groups, pad, parts,
           owner_h, cash_h, flags_h, rates_h, infl_h, returns_h, alloc_h, share_h, assets0_h, basis_h,
           book_ref, coef_ref, base_ref,
           owner_v, cash_v, flags_v, rates_v, infl_v, returns_v, alloc_v, share_v, assets0_v, basis_v,
           comp_send, comp_recv, flag_send, flag_recv, disc_v, held_send, held_recv,
           base_send, base_recv, claim_send, claim_recv,
           local_sem, comp_ss, comp_rs, flag_ss, flag_rs, held_ss, held_rs, base_ss, base_rs, claim_ss, claim_rs):
    g = lax.axis_index("scheme")
    c = lax.axis_index("scen")
    rows = owner_v.shape[1]
    years = rates_v.shape[1]
    hor = rates_v.shape[0]
    n = rates_v.shape[2]
    classes = returns_v.shape[1]

    def local(k, src, dst):
        copy = pltpu.make_async_copy(src, dst, local_sem.at[k])
        copy.start()
        return copy

    in_owner = local(0, owner_h, owner_v)
    in_flags = local(1, flags_h, flags_v)
    in_cash = local(2, cash_h, cash_v)
    in_rates = local(3, rates_h, rates_v)
    in_infl = local(4, infl_h, infl_v)
    in_returns = local(5, returns_h, returns_v)
    in_alloc = local(6, alloc_h, alloc_v)
    in_share = local(7, share_h, share_v)
    in_assets0 = local(8, assets0_h, assets0_v)
    in_basis = local(9, basis_h, basis_v)

    barrier = pltpu.get_barrier_semaphore()

    def greet(i):
        pl.semaphore_signal(barrier, inc=1, device_id={"scheme": lax.rem(g + i, groups)})

    def greet_scen(i):
        pl.semaphore_signal(barrier, inc=1, device_id={"scen": lax.rem(c + i, parts)})

    each(1, groups, greet)
    each(1, parts, greet_scen)

    def to_scheme(src, dst, ss, rs, i):
        return pltpu.make_async_remote_copy(
            src_ref=src, dst_ref=dst, send_sem=ss.at[i], recv_sem=rs.at[i],
            device_id={"scheme": lax.rem(g + i, groups)})

    def comp_copy(i):
        return to_scheme(comp_send.at[block(i, pad)], comp_recv.at[block(i, pad)], comp_ss, comp_rs, i)

    def flag_copy(i):
        return to_scheme(flag_send.at[block(i, pad)], flag_recv.at[block(i, pad)], flag_ss, flag_rs, i)

    def held_copy(i):
        return to_scheme(held_send.at[i], held_recv.at[i], held_ss, held_rs, i)

    def claim_copy(i):
        return to_scheme(claim_send, claim_recv.at[i], claim_ss, claim_rs, i)

    def base_copy(i):
        return pltpu.make_async_remote_copy(
            src_ref=base_send, dst_ref=base_recv.at[i], send_sem=base_ss.at[i], recv_sem=base_rs.at[i],
            device_id={"scen": lax.rem(c + i, parts)})

    in_owner.wait()
    rel = lax.rem(owner_v[...] - g + groups, groups)
    hits = (rel == lax.broadcasted_iota(jnp.int32, (groups, rows), 0)).astype(jnp.float32)
    upper = (lax.broadcasted_iota(jnp.int32, (rows, rows), 0)
             < lax.broadcasted_iota(jnp.int32, (rows, rows), 1)).astype(jnp.bfloat16)
    earlier = jnp.dot(hits.astype(jnp.bfloat16), upper, preferred_element_type=jnp.float32)
    rank = jnp.sum(earlier * hits, axis=0, keepdims=True).astype(jnp.int32)
    slot = rel * pad + rank
    pick = (slot == lax.broadcasted_iota(jnp.int32, (groups * pad, rows), 0)).astype(jnp.bfloat16)

    in_flags.wait()
    flags = [flags_v[:, y, :].astype(jnp.float32) for y in range(years)]
    for y in range(years):
        flag_send[:, y * n:(y + 1) * n] = jnp.dot(
            pick, flags[y].astype(jnp.bfloat16), preferred_element_type=jnp.float32).astype(jnp.bfloat16)
    in_cash.wait()
    cash_t = cash_v[...]
    comp_t = jnp.minimum(0.9 * cash_t.astype(jnp.float32), COMP_LIMIT).astype(jnp.bfloat16)
    comp_send[...] = lax.dot_general(
        pick, comp_t, NT, preferred_element_type=jnp.float32).astype(jnp.bfloat16)

    pl.semaphore_wait(barrier, groups + parts - 2)
    each(1, groups, lambda i: comp_copy(i).start())
    each(1, groups, lambda i: flag_copy(i).start())
    comp_recv[0:pad] = comp_send[0:pad]
    flag_recv[0:pad] = flag_send[0:pad]

    in_returns.wait()
    in_alloc.wait()
    in_share.wait()
    in_assets0.wait()
    eye = (lax.broadcasted_iota(jnp.int32, (rows, rows), 0)
           == lax.broadcasted_iota(jnp.int32, (rows, rows), 1))
    class_id = lax.broadcasted_iota(jnp.int32, (classes, rows), 0)
    exposure_t = jnp.zeros((classes, rows), jnp.float32)
    for j in range(alloc_v.shape[0]):
        exposure_t = exposure_t + jnp.where(alloc_v[j:j + 1, :] == class_id, share_v[j:j + 1, :], 0.0)
    assets = jnp.sum(jnp.where(eye, assets0_v[...], 0.0), axis=1, keepdims=True)
    held = []
    for y in range(years):
        growth = lax.dot_general(exposure_t, returns_v[y], TN, precision=HIGHEST,
                                 preferred_element_type=jnp.float32)
        assets = assets * jnp.exp(growth)
        held.append(assets)
        held_send[:, y, :] = jnp.dot(hits, flags[y] * assets, precision=HIGHEST,
                                     preferred_element_type=jnp.float32)
    each(1, groups, lambda i: held_copy(i).start())

    in_rates.wait()
    in_infl.wait()
    neg_terms = -(lax.broadcasted_iota(jnp.int32, (hor, n), 0) + 1).astype(jnp.float32)
    short = jnp.zeros((rows, n), jnp.float32)
    for y in range(years):
        rate = rates_v[:, y, :]
        infl = infl_v[:, y, :]
        for k, index in enumerate(TRANCHE_INDEX):
            disc_v[y, k * hor:(k + 1) * hor, :] = jnp.exp(neg_terms * (rate - index * infl))
        liab = lax.dot_general(cash_t, disc_v[y].astype(jnp.bfloat16), TN,
                               preferred_element_type=jnp.float32)
        short = short + (jnp.maximum(liab - held[y], 0.0) + 0.05 * liab)
    base_send[...] = lax.dot_general(jnp.ones((8, n), jnp.float32), short, NT, precision=HIGHEST,
                                     preferred_element_type=jnp.float32)
    each(1, parts, lambda i: base_copy(i).start())

    in_basis.wait()
    basis = basis_v[0].astype(jnp.float32)
    factors = [(basis * disc_v[y].astype(jnp.bfloat16).astype(jnp.float32)).astype(jnp.bfloat16)
               for y in range(years)]
    each(1, groups, lambda i: comp_copy(i).wait_recv())
    each(1, groups, lambda i: flag_copy(i).wait_recv())
    book = []
    for y in range(years):
        value = jnp.dot(comp_recv[...], factors[y], preferred_element_type=jnp.float32)
        weight = flag_recv[:, y * n:(y + 1) * n].astype(jnp.float32)
        book.append(jnp.sum(weight * value, axis=0, keepdims=True))
    each(1, groups, lambda i: held_copy(i).wait_recv())
    held_recv[0] = held_send[0]
    for y in range(years):
        book[y] = book[y] - jnp.sum(held_recv[:, y, :], axis=0, keepdims=True)
        claim_send[y:y + 1, :] = book[y]
        book_ref[0, y:y + 1, :] = book[y]

    each(1, parts, lambda i: base_copy(i).wait_recv())
    base = base_send[0:1, :]
    for i in range(1, parts):
        base = base + base_recv[i, 0:1, :]
    base = base / (n * parts * years)
    base_ref[...] = base
    claim_send[years:years + 1, :] = jnp.broadcast_to(jnp.sum(base, axis=1, keepdims=True), (1, n))
    each(1, groups, lambda i: claim_copy(i).start())
    claim_recv[0] = claim_send[...]
    each(1, groups, lambda i: claim_copy(i).wait_recv())
    total = jnp.sum(claim_recv[...], axis=0)
    for y in range(years):
        coef_ref[y:y + 1, :] = (total[y:y + 1, :] / groups) / (total[years:years + 1, :] / (rows * groups))

    each(1, groups, lambda i: comp_copy(i).wait_send())
    each(1, groups, lambda i: flag_copy(i).wait_send())
    each(1, groups, lambda i: held_copy(i).wait_send())
    each(1, parts, lambda i: base_copy(i).wait_send())
    each(1, groups, lambda i: claim_copy(i).wait_send())


def shards(cashflow, assets0, alloc, share, owner, flags, rates, inflation, returns, basis):
    rows, width = cashflow.shape
    years, hor, n = rates.shape
    classes = returns.shape[1]
    hold = alloc.shape[1]
    groups = lax.axis_size("scheme")
    parts = lax.axis_size("scen")
    cap = max(2, (2 * rows + groups - 1) // groups)
    pad = -(-cap // 16) * 16
    f32, bf16, i32 = jnp.float32, jnp.bfloat16, jnp.int32
    dma = pltpu.SemaphoreType.DMA
    book, coef, base = pl.pallas_call(
        functools.partial(kernel, groups, pad, parts),
        out_shape=(jax.ShapeDtypeStruct((1, years, n), f32),
                   jax.ShapeDtypeStruct((years, n), f32),
                   jax.ShapeDtypeStruct((1, rows), f32)),
        in_specs=[pl.BlockSpec(memory_space=pl.ANY)] * 10,
        out_specs=(pl.BlockSpec(memory_space=pltpu.VMEM),) * 3,
        scratch_shapes=[
            pltpu.VMEM((1, rows), i32),
            pltpu.VMEM((width, rows), bf16),
            pltpu.VMEM((rows, years, n), i32),
            pltpu.VMEM((hor, years, n), f32),
            pltpu.VMEM((hor, years, n), f32),
            pltpu.VMEM((years, classes, n), f32),
            pltpu.VMEM((hold, rows), i32),
            pltpu.VMEM((hold, rows), f32),
            pltpu.VMEM((1, rows), f32),
            pltpu.VMEM((1, width, n), bf16),
            pltpu.VMEM((groups * pad, width), bf16),
            pltpu.VMEM((groups * pad, width), bf16),
            pltpu.VMEM((groups * pad, years * n), bf16),
            pltpu.VMEM((groups * pad, years * n), bf16),
            pltpu.VMEM((years, width, n), f32),
            pltpu.VMEM((groups, years, n), f32),
            pltpu.VMEM((groups, years, n), f32),
            pltpu.VMEM((8, rows), f32),
            pltpu.VMEM((parts, 8, rows), f32),
            pltpu.VMEM((years + 1, n), f32),
            pltpu.VMEM((groups, years + 1, n), f32),
            dma((10,)),
            dma((groups,)), dma((groups,)),
            dma((groups,)), dma((groups,)),
            dma((groups,)), dma((groups,)),
            dma((parts,)), dma((parts,)),
            dma((groups,)), dma((groups,)),
        ],
        compiler_params=pltpu.CompilerParams(
            collective_id=0, has_side_effects=True, vmem_limit_bytes=48 * 2**20),
        name="fund",
    )(owner.T, cashflow.T, flags, rates.transpose(1, 0, 2), inflation.transpose(1, 0, 2), returns,
      alloc.T, share.T, assets0.reshape(1, rows), basis)
    levy = coef[None] * base.reshape(rows, 1, 1)
    return book, levy


def solution(mesh):
    placed = (
        P("scheme", None),
        P("scheme"),
        P("scheme", None),
        P("scheme", None),
        P("scheme", None),
        P("scheme", None, "scen"),
        P(None, None, "scen"),
        P(None, None, "scen"),
        P(None, None, "scen"),
        P("scheme", None, "scen"),
    )
    return jax.shard_map(
        shards,
        mesh=mesh,
        in_specs=placed,
        out_specs=(P("scheme", None, "scen"), P("scheme", None, "scen")),
        check_vma=False,
    )
```

```python
import functools

import jax
import jax.numpy as jnp
from jax import lax
from jax.experimental import pallas as pl
from jax.experimental.pallas import tpu as pltpu
from jax.sharding import PartitionSpec as P

TRANCHE_INDEX = (0.0, 0.5, 1.0, 0.75)
COMP_LIMIT = 0.004
HIGHEST = lax.Precision.HIGHEST
NT = (((1,), (1,)), ((), ()))
TN = (((0,), (0,)), ((), ()))


def each(low, high, body):
    if high - low <= 16:
        for i in range(low, high):
            body(i)
    else:
        lax.fori_loop(low, high, lambda i, c: (body(i), c)[1], 0)


def block(i, size):
    start = i * size
    return pl.ds(start if isinstance(start, int) else pl.multiple_of(start, size), size)


def kernel(groups, pad, parts,
           owner_h, cash_h, flags_h, rates_h, infl_h, returns_h, alloc_h, share_h, assets0_h, basis_h,
           book_ref, coef_ref, base_ref,
           owner_v, cash_v, flags_v, rates_v, infl_v, returns_v, alloc_v, share_v, assets0_v, basis_v,
           comp_send, comp_recv, flag_send, flag_recv, disc_v, held_send, held_recv,
           base_send, base_recv, claim_send, claim_recv,
           value_v, strip_ss, strip_rs,
           local_sem, comp_ss, comp_rs, flag_ss, flag_rs, held_ss, held_rs, base_ss, base_rs, claim_ss, claim_rs):
    g = lax.axis_index("scheme")
    c = lax.axis_index("scen")
    rows = owner_v.shape[1]
    years = rates_v.shape[1]
    hor = rates_v.shape[0]
    n = rates_v.shape[2]
    classes = returns_v.shape[1]
    width = cash_v.shape[0]
    lanes = comp_send.shape[1] // parts
    mine = block(c, lanes)

    def local(k, src, dst):
        copy = pltpu.make_async_copy(src, dst, local_sem.at[k])
        copy.start()
        return copy

    in_owner = local(0, owner_h, owner_v)
    in_flags = local(1, flags_h, flags_v)
    in_cash = local(2, cash_h, cash_v)
    in_rates = local(3, rates_h, rates_v)
    in_infl = local(4, infl_h, infl_v)
    in_returns = local(5, returns_h, returns_v)
    in_alloc = local(6, alloc_h, alloc_v)
    in_share = local(7, share_h, share_v)
    in_assets0 = local(8, assets0_h, assets0_v)
    in_basis = local(9, basis_h, basis_v)

    barrier = pltpu.get_barrier_semaphore()

    def greet(i):
        pl.semaphore_signal(barrier, inc=1, device_id={"scheme": lax.rem(g + i, groups)})

    def greet_scen(i):
        pl.semaphore_signal(barrier, inc=1, device_id={"scen": lax.rem(c + i, parts)})

    each(1, groups, greet)
    each(1, parts, greet_scen)

    def to_scheme(src, dst, ss, rs, i):
        return pltpu.make_async_remote_copy(
            src_ref=src, dst_ref=dst, send_sem=ss.at[i], recv_sem=rs.at[i],
            device_id={"scheme": lax.rem(g + i, groups)})

    def comp_copy(i):
        return to_scheme(comp_send.at[block(i, pad), mine], comp_recv.at[block(i, pad), mine], comp_ss, comp_rs, i)

    def strip_copy(i):
        return pltpu.make_async_remote_copy(
            src_ref=comp_recv.at[pad:, mine], dst_ref=comp_recv.at[pad:, mine],
            send_sem=strip_ss.at[i], recv_sem=strip_rs.at[i],
            device_id={"scen": lax.rem(c + i, parts)})

    def strip_arrival(i):
        strip = comp_recv.at[pad:, block(lax.rem(c - i + parts, parts), lanes)]
        return pltpu.make_async_remote_copy(
            src_ref=strip, dst_ref=strip,
            send_sem=strip_ss.at[i], recv_sem=strip_rs.at[i],
            device_id={"scen": lax.rem(c + i, parts)})

    def flag_copy(i):
        return to_scheme(flag_send.at[block(i, pad)], flag_recv.at[block(i, pad)], flag_ss, flag_rs, i)

    def held_copy(i):
        return to_scheme(held_send.at[i], held_recv.at[i], held_ss, held_rs, i)

    def claim_copy(i):
        return to_scheme(claim_send, claim_recv.at[i], claim_ss, claim_rs, i)

    def base_copy(i):
        return pltpu.make_async_remote_copy(
            src_ref=base_send, dst_ref=base_recv.at[i], send_sem=base_ss.at[i], recv_sem=base_rs.at[i],
            device_id={"scen": lax.rem(c + i, parts)})

    in_owner.wait()
    rel = lax.rem(owner_v[...] - g + groups, groups)
    hits = (rel == lax.broadcasted_iota(jnp.int32, (groups, rows), 0)).astype(jnp.float32)
    upper = (lax.broadcasted_iota(jnp.int32, (rows, rows), 0)
             < lax.broadcasted_iota(jnp.int32, (rows, rows), 1)).astype(jnp.bfloat16)
    earlier = jnp.dot(hits.astype(jnp.bfloat16), upper, preferred_element_type=jnp.float32)
    rank = jnp.sum(earlier * hits, axis=0, keepdims=True).astype(jnp.int32)
    slot = rel * pad + rank
    pick = (slot == lax.broadcasted_iota(jnp.int32, (groups * pad, rows), 0)).astype(jnp.bfloat16)

    in_cash.wait()
    cash_t = cash_v[...]
    comp_t = jnp.minimum(0.9 * cash_t.astype(jnp.float32), COMP_LIMIT).astype(jnp.bfloat16)
    comp_rows = lax.dot_general(pick, comp_t, NT, preferred_element_type=jnp.float32).astype(jnp.bfloat16)
    comp_send[:, :width] = comp_rows
    if comp_send.shape[1] > width:
        comp_send[:, width:] = jnp.zeros((comp_send.shape[0], comp_send.shape[1] - width), jnp.bfloat16)

    pl.semaphore_wait(barrier, groups + parts - 2)
    each(1, groups, lambda i: comp_copy(i).start())
    comp_recv[0:pad, :width] = comp_rows[0:pad]

    in_flags.wait()
    flags = [flags_v[:, y, :].astype(jnp.float32) for y in range(years)]
    for y in range(years):
        flag_send[:, y * n:(y + 1) * n] = jnp.dot(
            pick, flags[y].astype(jnp.bfloat16), preferred_element_type=jnp.float32).astype(jnp.bfloat16)
    each(1, groups, lambda i: flag_copy(i).start())

    in_returns.wait()
    in_alloc.wait()
    in_share.wait()
    in_assets0.wait()
    eye = (lax.broadcasted_iota(jnp.int32, (rows, rows), 0)
           == lax.broadcasted_iota(jnp.int32, (rows, rows), 1))
    class_id = lax.broadcasted_iota(jnp.int32, (classes, rows), 0)
    exposure_t = jnp.zeros((classes, rows), jnp.float32)
    for j in range(alloc_v.shape[0]):
        exposure_t = exposure_t + jnp.where(alloc_v[j:j + 1, :] == class_id, share_v[j:j + 1, :], 0.0)
    assets = jnp.sum(jnp.where(eye, assets0_v[...], 0.0), axis=1, keepdims=True)
    held = []
    for y in range(years):
        growth = lax.dot_general(exposure_t, returns_v[y], TN, precision=HIGHEST,
                                 preferred_element_type=jnp.float32)
        assets = assets * jnp.exp(growth)
        held.append(assets)
        held_send[:, y, :] = jnp.dot(hits, flags[y] * assets, precision=HIGHEST,
                                     preferred_element_type=jnp.float32)
    each(1, groups, lambda i: held_copy(i).start())

    each(1, groups, lambda i: comp_copy(i).wait_recv())
    each(1, parts, lambda i: strip_copy(i).start())

    in_rates.wait()
    in_infl.wait()
    neg_terms = -(lax.broadcasted_iota(jnp.int32, (hor, n), 0) + 1).astype(jnp.float32)
    short = jnp.zeros((rows, n), jnp.float32)
    for y in range(years):
        rate = rates_v[:, y, :]
        infl = infl_v[:, y, :]
        for k, index in enumerate(TRANCHE_INDEX):
            disc_v[y, k * hor:(k + 1) * hor, :] = jnp.exp(neg_terms * (rate - index * infl))
        liab = lax.dot_general(cash_t, disc_v[y].astype(jnp.bfloat16), TN,
                               preferred_element_type=jnp.float32)
        short = short + (jnp.maximum(liab - held[y], 0.0) + 0.05 * liab)
    base_send[...] = lax.dot_general(jnp.ones((8, n), jnp.float32), short, NT, precision=HIGHEST,
                                     preferred_element_type=jnp.float32)
    each(1, parts, lambda i: base_copy(i).start())

    in_basis.wait()
    basis = basis_v[0].astype(jnp.float32)
    factors = [(basis * disc_v[y].astype(jnp.bfloat16).astype(jnp.float32)).astype(jnp.bfloat16)
               for y in range(years)]
    each(1, parts, lambda i: strip_arrival(i).wait_recv())
    for y in range(years):
        value_v[:, y * n:(y + 1) * n] = jnp.dot(comp_recv[:, :width], factors[y],
                                                preferred_element_type=jnp.float32)
    value_v[0:pad] = flag_send[0:pad].astype(jnp.float32) * value_v[0:pad]

    def add_book(i):
        flag_copy(i).wait_recv()
        at = block(i, pad)
        value_v[0:pad] = value_v[0:pad] + flag_recv[at].astype(jnp.float32) * value_v[at]

    each(1, groups, add_book)
    summed = jnp.sum(value_v[0:pad], axis=0, keepdims=True)
    book = [summed[:, y * n:(y + 1) * n] for y in range(years)]
    each(1, groups, lambda i: held_copy(i).wait_recv())
    held_recv[0] = held_send[0]
    for y in range(years):
        book[y] = book[y] - jnp.sum(held_recv[:, y, :], axis=0, keepdims=True)
        claim_send[y:y + 1, :] = book[y]
        book_ref[0, y:y + 1, :] = book[y]

    each(1, parts, lambda i: base_copy(i).wait_recv())
    base = base_send[0:1, :]
    for i in range(1, parts):
        base = base + base_recv[i, 0:1, :]
    base = base / (n * parts * years)
    base_ref[...] = base
    claim_send[years:years + 1, :] = jnp.broadcast_to(jnp.sum(base, axis=1, keepdims=True), (1, n))
    each(1, groups, lambda i: claim_copy(i).start())
    claim_recv[0] = claim_send[...]
    each(1, groups, lambda i: claim_copy(i).wait_recv())
    total = jnp.sum(claim_recv[...], axis=0)
    for y in range(years):
        coef_ref[y:y + 1, :] = (total[y:y + 1, :] / groups) / (total[years:years + 1, :] / (rows * groups))

    each(1, groups, lambda i: comp_copy(i).wait_send())
    each(1, parts, lambda i: strip_copy(i).wait_send())
    each(1, groups, lambda i: flag_copy(i).wait_send())
    each(1, groups, lambda i: held_copy(i).wait_send())
    each(1, parts, lambda i: base_copy(i).wait_send())
    each(1, groups, lambda i: claim_copy(i).wait_send())


def shards(cashflow, assets0, alloc, share, owner, flags, rates, inflation, returns, basis):
    rows, width = cashflow.shape
    years, hor, n = rates.shape
    classes = returns.shape[1]
    hold = alloc.shape[1]
    groups = lax.axis_size("scheme")
    parts = lax.axis_size("scen")
    cap = max(2, (2 * rows + groups - 1) // groups)
    pad = -(-cap // 16) * 16
    lanes = -(-width // (128 * parts)) * 128
    f32, bf16, i32 = jnp.float32, jnp.bfloat16, jnp.int32
    dma = pltpu.SemaphoreType.DMA
    book, coef, base = pl.pallas_call(
        functools.partial(kernel, groups, pad, parts),
        out_shape=(jax.ShapeDtypeStruct((1, years, n), f32),
                   jax.ShapeDtypeStruct((years, n), f32),
                   jax.ShapeDtypeStruct((1, rows), f32)),
        in_specs=[pl.BlockSpec(memory_space=pltpu.HBM)] * 10,
        out_specs=(pl.BlockSpec(memory_space=pltpu.VMEM),) * 3,
        scratch_shapes=[
            pltpu.VMEM((1, rows), i32),
            pltpu.VMEM((width, rows), bf16),
            pltpu.VMEM((rows, years, n), i32),
            pltpu.VMEM((hor, years, n), f32),
            pltpu.VMEM((hor, years, n), f32),
            pltpu.VMEM((years, classes, n), f32),
            pltpu.VMEM((hold, rows), i32),
            pltpu.VMEM((hold, rows), f32),
            pltpu.VMEM((1, rows), f32),
            pltpu.VMEM((1, width, n), bf16),
            pltpu.VMEM((groups * pad, parts * lanes), bf16),
            pltpu.VMEM((groups * pad, parts * lanes), bf16),
            pltpu.VMEM((groups * pad, years * n), bf16),
            pltpu.VMEM((groups * pad, years * n), bf16),
            pltpu.VMEM((years, width, n), f32),
            pltpu.VMEM((groups, years, n), f32),
            pltpu.VMEM((groups, years, n), f32),
            pltpu.VMEM((8, rows), f32),
            pltpu.VMEM((parts, 8, rows), f32),
            pltpu.VMEM((years + 1, n), f32),
            pltpu.VMEM((groups, years + 1, n), f32),
            pltpu.VMEM((groups * pad, years * n), f32),
            dma((parts,)), dma((parts,)),
            dma((10,)),
            dma((groups,)), dma((groups,)),
            dma((groups,)), dma((groups,)),
            dma((groups,)), dma((groups,)),
            dma((parts,)), dma((parts,)),
            dma((groups,)), dma((groups,)),
        ],
        compiler_params=pltpu.CompilerParams(
            collective_id=0, has_side_effects=True, vmem_limit_bytes=60 * 2**20),
        name="fund",
    )(owner.T, cashflow.T, flags, rates.transpose(1, 0, 2), inflation.transpose(1, 0, 2), returns,
      alloc.T, share.T, assets0.reshape(1, rows), basis)
    levy = coef[None] * base.reshape(rows, 1, 1)
    return book, levy


def solution(mesh):
    placed = (
        P("scheme", None),
        P("scheme"),
        P("scheme", None),
        P("scheme", None),
        P("scheme", None),
        P("scheme", None, "scen"),
        P(None, None, "scen"),
        P(None, None, "scen"),
        P(None, None, "scen"),
        P("scheme", None, "scen"),
    )
    return jax.shard_map(
        shards,
        mesh=mesh,
        in_specs=placed,
        out_specs=(P("scheme", None, "scen"), P("scheme", None, "scen")),
        check_vma=False,
    )
```

```python
import functools

import jax
import jax.numpy as jnp
from jax import lax
from jax.experimental import pallas as pl
from jax.experimental.pallas import tpu as pltpu
from jax.sharding import PartitionSpec as P

TRANCHE_INDEX = (0.0, 0.5, 1.0, 0.75)
COMP_LIMIT = 0.004
HIGHEST = lax.Precision.HIGHEST
NT = (((1,), (1,)), ((), ()))
TN = (((0,), (0,)), ((), ()))


def each(low, high, body):
    if high - low <= 16:
        for i in range(low, high):
            body(i)
    else:
        lax.fori_loop(low, high, lambda i, c: (body(i), c)[1], 0)


def pieces(x):
    high = x.astype(jnp.bfloat16)
    rest = x - high.astype(jnp.float32)
    middle = rest.astype(jnp.bfloat16)
    low = (rest - middle.astype(jnp.float32)).astype(jnp.bfloat16)
    return high, middle, low


def block(i, size):
    start = i * size
    return pl.ds(start if isinstance(start, int) else pl.multiple_of(start, size), size)


def kernel(groups, pad, parts,
           owner_h, cash_h, flags_h, rates_h, infl_h, returns_h, alloc_h, share_h, assets0_h, basis_h,
           book_ref, coef_ref, base_ref,
           owner_v, cash_v, flags_v, rates_v, infl_v, returns_v, alloc_v, share_v, assets0_v, basis_v,
           comp_send, comp_recv, flag_send, flag_recv, disc_v, held_send, held_recv,
           base_send, base_recv, claim_send, claim_recv,
           value_v, strip_ss, strip_rs,
           local_sem, comp_ss, comp_rs, flag_ss, flag_rs, held_ss, held_rs, base_ss, base_rs, claim_ss, claim_rs):
    g = lax.axis_index("scheme")
    c = lax.axis_index("scen")
    rows = owner_v.shape[1]
    years = rates_v.shape[1]
    hor = rates_v.shape[0]
    n = rates_v.shape[2]
    classes = returns_v.shape[1]
    width = cash_v.shape[0]
    lanes = comp_send.shape[1] // parts
    mine = block(c, lanes)

    def local(k, src, dst):
        copy = pltpu.make_async_copy(src, dst, local_sem.at[k])
        copy.start()
        return copy

    in_owner = local(0, owner_h, owner_v)
    in_cash = local(2, cash_h, cash_v)
    in_flags = local(1, flags_h, flags_v)
    in_rates = local(3, rates_h, rates_v)
    in_infl = local(4, infl_h, infl_v)
    in_returns = local(5, returns_h, returns_v)
    in_alloc = local(6, alloc_h, alloc_v)
    in_share = local(7, share_h, share_v)
    in_assets0 = local(8, assets0_h, assets0_v)
    in_basis = local(9, basis_h, basis_v)

    barrier = pltpu.get_barrier_semaphore()

    def greet(i):
        pl.semaphore_signal(barrier, inc=1, device_id={"scheme": lax.rem(g + i, groups)})

    def greet_scen(i):
        pl.semaphore_signal(barrier, inc=1, device_id={"scen": lax.rem(c + i, parts)})

    each(1, groups, greet)
    each(1, parts, greet_scen)

    def to_scheme(src, dst, ss, rs, i):
        return pltpu.make_async_remote_copy(
            src_ref=src, dst_ref=dst, send_sem=ss.at[i], recv_sem=rs.at[i],
            device_id={"scheme": lax.rem(g + i, groups)})

    def comp_copy(i):
        return to_scheme(comp_send.at[block(i, pad), mine], comp_recv.at[block(i, pad), mine], comp_ss, comp_rs, i)

    def strip_copy(i):
        return pltpu.make_async_remote_copy(
            src_ref=comp_recv.at[pad:, mine], dst_ref=comp_recv.at[pad:, mine],
            send_sem=strip_ss.at[i], recv_sem=strip_rs.at[i],
            device_id={"scen": lax.rem(c + i, parts)})

    def strip_arrival(i):
        strip = comp_recv.at[pad:, block(lax.rem(c - i + parts, parts), lanes)]
        return pltpu.make_async_remote_copy(
            src_ref=strip, dst_ref=strip,
            send_sem=strip_ss.at[i], recv_sem=strip_rs.at[i],
            device_id={"scen": lax.rem(c + i, parts)})

    def flag_copy(i):
        return to_scheme(flag_send.at[block(i, pad)], flag_recv.at[block(i, pad)], flag_ss, flag_rs, i)

    def held_copy(i):
        return to_scheme(held_send.at[i], held_recv.at[i], held_ss, held_rs, i)

    def claim_copy(i):
        return to_scheme(claim_send, claim_recv.at[i], claim_ss, claim_rs, i)

    def base_copy(i):
        return pltpu.make_async_remote_copy(
            src_ref=base_send, dst_ref=base_recv.at[i], send_sem=base_ss.at[i], recv_sem=base_rs.at[i],
            device_id={"scen": lax.rem(c + i, parts)})

    in_owner.wait()
    rel = lax.rem(owner_v[...] - g + groups, groups)
    hits = (rel == lax.broadcasted_iota(jnp.int32, (groups, rows), 0)).astype(jnp.float32)
    upper = (lax.broadcasted_iota(jnp.int32, (rows, rows), 0)
             < lax.broadcasted_iota(jnp.int32, (rows, rows), 1)).astype(jnp.bfloat16)
    hits_b = hits.astype(jnp.bfloat16)
    earlier = jnp.dot(hits_b, upper, preferred_element_type=jnp.float32)
    rank = jnp.sum(earlier * hits, axis=0, keepdims=True).astype(jnp.int32)
    slot = rel * pad + rank
    pick = (slot == lax.broadcasted_iota(jnp.int32, (groups * pad, rows), 0)).astype(jnp.bfloat16)

    in_cash.wait()
    cash_t = cash_v[...]
    comp_t = jnp.minimum(0.9 * cash_t.astype(jnp.float32), COMP_LIMIT).astype(jnp.bfloat16)
    comp_rows = lax.dot_general(pick, comp_t, NT, preferred_element_type=jnp.float32).astype(jnp.bfloat16)
    comp_send[:, :width] = comp_rows
    if comp_send.shape[1] > width:
        comp_send[:, width:] = jnp.zeros((comp_send.shape[0], comp_send.shape[1] - width), jnp.bfloat16)

    pl.semaphore_wait(barrier, groups + parts - 2)
    each(1, groups, lambda i: comp_copy(i).start())
    comp_recv[0:pad, :width] = comp_rows[0:pad]

    in_flags.wait()
    flags = [flags_v[:, y, :].astype(jnp.float32) for y in range(years)]
    for y in range(years):
        flag_send[:, y * n:(y + 1) * n] = jnp.dot(
            pick, flags[y].astype(jnp.bfloat16), preferred_element_type=jnp.float32).astype(jnp.bfloat16)
    each(1, groups, lambda i: flag_copy(i).start())

    in_returns.wait()
    in_alloc.wait()
    in_share.wait()
    in_assets0.wait()
    eye = (lax.broadcasted_iota(jnp.int32, (rows, rows), 0)
           == lax.broadcasted_iota(jnp.int32, (rows, rows), 1))
    class_id = lax.broadcasted_iota(jnp.int32, (classes, rows), 0)
    exposure_t = jnp.zeros((classes, rows), jnp.float32)
    for j in range(alloc_v.shape[0]):
        exposure_t = exposure_t + jnp.where(alloc_v[j:j + 1, :] == class_id, share_v[j:j + 1, :], 0.0)
    assets = jnp.sum(jnp.where(eye, assets0_v[...], 0.0), axis=1, keepdims=True)
    held = []
    for y in range(years):
        growth = lax.dot_general(exposure_t, returns_v[y], TN, precision=HIGHEST,
                                 preferred_element_type=jnp.float32)
        assets = assets * jnp.exp(growth)
        held.append(assets)
        held_send[:, y, :] = sum(jnp.dot(hits_b, piece, preferred_element_type=jnp.float32)
                                 for piece in pieces(flags[y] * assets))
    each(1, groups, lambda i: held_copy(i).start())


    in_rates.wait()
    in_infl.wait()
    neg_terms = -(lax.broadcasted_iota(jnp.int32, (hor, n), 0) + 1).astype(jnp.float32)
    short = jnp.zeros((rows, n), jnp.float32)
    for y in range(years):
        rate = rates_v[:, y, :]
        infl = infl_v[:, y, :]
        for k, index in enumerate(TRANCHE_INDEX):
            disc_v[y, k * hor:(k + 1) * hor, :] = jnp.exp(neg_terms * (rate - index * infl))
        liab = lax.dot_general(cash_t, disc_v[y].astype(jnp.bfloat16), TN,
                               preferred_element_type=jnp.float32)
        short = short + (jnp.maximum(liab - held[y], 0.0) + 0.05 * liab)
    each(1, groups, lambda i: comp_copy(i).wait_recv())
    each(1, parts, lambda i: strip_copy(i).start())
    base_send[...] = jnp.sum(jnp.where(eye, jnp.sum(short, axis=1, keepdims=True), 0.0), axis=0, keepdims=True)
    each(1, parts, lambda i: base_copy(i).start())

    in_basis.wait()
    basis = basis_v[0].astype(jnp.float32)
    factors = [(basis * disc_v[y].astype(jnp.bfloat16).astype(jnp.float32)).astype(jnp.bfloat16)
               for y in range(years)]
    each(1, parts, lambda i: strip_arrival(i).wait_recv())
    for y in range(years):
        value_v[:, y * n:(y + 1) * n] = jnp.dot(comp_recv[:, :width], factors[y],
                                                preferred_element_type=jnp.float32)
    value_v[0:pad] = flag_send[0:pad].astype(jnp.float32) * value_v[0:pad]

    def add_book(i):
        flag_copy(i).wait_recv()
        at = block(i, pad)
        value_v[0:pad] = value_v[0:pad] + flag_recv[at].astype(jnp.float32) * value_v[at]

    each(1, groups, add_book)
    summed = jnp.sum(value_v[0:pad], axis=0, keepdims=True)
    book = [summed[:, y * n:(y + 1) * n] for y in range(years)]
    each(1, groups, lambda i: held_copy(i).wait_recv())
    held_recv[0] = held_send[0]
    for y in range(years):
        book[y] = book[y] - jnp.sum(held_recv[:, y, :], axis=0, keepdims=True)
        claim_send[y:y + 1, :] = book[y]
        book_ref[0, y:y + 1, :] = book[y]

    each(1, parts, lambda i: base_copy(i).wait_recv())
    base = base_send[...]
    for i in range(1, parts):
        base = base + base_recv[i]
    base = base / (n * parts * years)
    base_ref[...] = base
    claim_send[years:years + 1, :] = jnp.broadcast_to(jnp.sum(base, axis=1, keepdims=True), (1, n))
    each(1, groups, lambda i: claim_copy(i).start())
    claim_recv[0] = claim_send[...]
    each(1, groups, lambda i: claim_copy(i).wait_recv())
    total = jnp.sum(claim_recv[...], axis=0)
    for y in range(years):
        coef_ref[y:y + 1, :] = (total[y:y + 1, :] / groups) / (total[years:years + 1, :] / (rows * groups))

    each(1, groups, lambda i: comp_copy(i).wait_send())
    each(1, parts, lambda i: strip_copy(i).wait_send())
    each(1, groups, lambda i: flag_copy(i).wait_send())
    each(1, groups, lambda i: held_copy(i).wait_send())
    each(1, parts, lambda i: base_copy(i).wait_send())
    each(1, groups, lambda i: claim_copy(i).wait_send())


def spread(book_in, coef_ref, base_ref, book_ref, levy_ref):
    rows, years, n = levy_ref.shape
    eye = (lax.broadcasted_iota(jnp.int32, (rows, rows), 0)
           == lax.broadcasted_iota(jnp.int32, (rows, rows), 1))
    base = jnp.sum(jnp.where(eye, base_ref[...], 0.0), axis=1, keepdims=True)
    book_ref[...] = book_in[...]
    for y in range(years):
        levy_ref[:, y, :] = coef_ref[y:y + 1, :] * base


def shards(cashflow, assets0, alloc, share, owner, flags, rates, inflation, returns, basis):
    rows, width = cashflow.shape
    years, hor, n = rates.shape
    classes = returns.shape[1]
    hold = alloc.shape[1]
    groups = lax.axis_size("scheme")
    parts = lax.axis_size("scen")
    cap = max(2, (2 * rows + groups - 1) // groups)
    pad = -(-cap // 16) * 16
    lanes = -(-width // (128 * parts)) * 128
    f32, bf16, i32 = jnp.float32, jnp.bfloat16, jnp.int32
    dma = pltpu.SemaphoreType.DMA
    book, coef, base = pl.pallas_call(
        functools.partial(kernel, groups, pad, parts),
        out_shape=(jax.ShapeDtypeStruct((1, years, n), f32),
                   jax.ShapeDtypeStruct((years, n), f32),
                   jax.ShapeDtypeStruct((1, rows), f32)),
        in_specs=[pl.BlockSpec(memory_space=pltpu.HBM)] * 10,
        out_specs=(pl.BlockSpec(memory_space=pltpu.VMEM),) * 3,
        scratch_shapes=[
            pltpu.VMEM((1, rows), i32),
            pltpu.VMEM((width, rows), bf16),
            pltpu.VMEM((rows, years, n), i32),
            pltpu.VMEM((hor, years, n), f32),
            pltpu.VMEM((hor, years, n), f32),
            pltpu.VMEM((years, classes, n), f32),
            pltpu.VMEM((hold, rows), i32),
            pltpu.VMEM((hold, rows), f32),
            pltpu.VMEM((1, rows), f32),
            pltpu.VMEM((1, width, n), bf16),
            pltpu.VMEM((groups * pad, parts * lanes), bf16),
            pltpu.VMEM((groups * pad, parts * lanes), bf16),
            pltpu.VMEM((groups * pad, years * n), bf16),
            pltpu.VMEM((groups * pad, years * n), bf16),
            pltpu.VMEM((years, width, n), f32),
            pltpu.VMEM((groups, years, n), f32),
            pltpu.VMEM((groups, years, n), f32),
            pltpu.VMEM((1, rows), f32),
            pltpu.VMEM((parts, 1, rows), f32),
            pltpu.VMEM((years + 1, n), f32),
            pltpu.VMEM((groups, years + 1, n), f32),
            pltpu.VMEM((groups * pad, years * n), f32),
            dma((parts,)), dma((parts,)),
            dma((10,)),
            dma((groups,)), dma((groups,)),
            dma((groups,)), dma((groups,)),
            dma((groups,)), dma((groups,)),
            dma((parts,)), dma((parts,)),
            dma((groups,)), dma((groups,)),
        ],
        compiler_params=pltpu.CompilerParams(
            collective_id=0, has_side_effects=True, vmem_limit_bytes=40 * 2**20),
        name="fund",
    )(*(pltpu.with_memory_space_constraint(x, pltpu.HBM) for x in (
        owner.T, cashflow.T, flags, rates.transpose(1, 0, 2), inflation.transpose(1, 0, 2), returns,
        alloc.T, share.T, assets0.reshape(1, rows), basis)))
    book, levy = pl.pallas_call(
        spread,
        out_shape=(jax.ShapeDtypeStruct((1, years, n), f32), jax.ShapeDtypeStruct((rows, years, n), f32)),
        in_specs=[pl.BlockSpec(memory_space=pltpu.VMEM)] * 3,
        out_specs=(pl.BlockSpec(memory_space=pltpu.VMEM),) * 2,
        compiler_params=pltpu.CompilerParams(vmem_limit_bytes=4 * 2**20),
        name="spread",
    )(book, coef, base)
    return book, levy


def solution(mesh):
    placed = (
        P("scheme", None),
        P("scheme"),
        P("scheme", None),
        P("scheme", None),
        P("scheme", None),
        P("scheme", None, "scen"),
        P(None, None, "scen"),
        P(None, None, "scen"),
        P(None, None, "scen"),
        P("scheme", None, "scen"),
    )
    return jax.shard_map(
        shards,
        mesh=mesh,
        in_specs=placed,
        out_specs=(P("scheme", None, "scen"), P("scheme", None, "scen")),
        check_vma=False,
    )
```

```python
import functools

import jax
import jax.numpy as jnp
from jax import lax
from jax.experimental import pallas as pl
from jax.experimental.pallas import tpu as pltpu
from jax.sharding import PartitionSpec as P

TRANCHE_INDEX = (0.0, 0.5, 1.0, 0.75)
COMP_LIMIT = 0.004
HIGHEST = lax.Precision.HIGHEST
NT = (((1,), (1,)), ((), ()))
TN = (((0,), (0,)), ((), ()))


def each(low, high, body):
    if high - low <= 16:
        for i in range(low, high):
            body(i)
    else:
        lax.fori_loop(low, high, lambda i, c: (body(i), c)[1], 0)


def pieces(x):
    high = x.astype(jnp.bfloat16)
    rest = x - high.astype(jnp.float32)
    middle = rest.astype(jnp.bfloat16)
    low = (rest - middle.astype(jnp.float32)).astype(jnp.bfloat16)
    return high, middle, low


def block(i, size):
    start = i * size
    return pl.ds(start if isinstance(start, int) else pl.multiple_of(start, size), size)


def kernel(groups, pad, parts,
           owner_h, cash_h, flags_h, rates_h, infl_h, returns_h, alloc_h, share_h, assets0_h, basis_h,
           book_ref, coef_ref, base_ref,
           owner_v, cash_v, flags_v, rates_v, infl_v, returns_v, alloc_v, share_v, assets0_v, basis_v,
           comp_send, comp_recv, flag_send, flag_recv, disc_v, held_send, held_recv,
           base_send, base_recv, claim_send, claim_recv,
           value_v, strip_ss, strip_rs,
           local_sem, comp_ss, comp_rs, flag_ss, flag_rs, held_ss, held_rs, base_ss, base_rs, claim_ss, claim_rs):
    g = lax.axis_index("scheme")
    c = lax.axis_index("scen")
    rows = owner_v.shape[1]
    years = rates_v.shape[1]
    hor = rates_v.shape[0]
    n = rates_v.shape[2]
    classes = returns_v.shape[1]
    width = cash_v.shape[0]
    lanes = comp_send.shape[1] // parts
    mine = block(c, lanes)

    def local(k, src, dst):
        copy = pltpu.make_async_copy(src, dst, local_sem.at[k])
        copy.start()
        return copy

    in_owner = local(0, owner_h, owner_v)
    in_cash = local(2, cash_h, cash_v)
    in_flags = local(1, flags_h, flags_v)
    in_rates = local(3, rates_h, rates_v)
    in_infl = local(4, infl_h, infl_v)
    in_returns = local(5, returns_h, returns_v)
    in_alloc = local(6, alloc_h, alloc_v)
    in_share = local(7, share_h, share_v)
    in_assets0 = local(8, assets0_h, assets0_v)
    in_basis = local(9, basis_h, basis_v)

    barrier = pltpu.get_barrier_semaphore()

    def greet(i):
        pl.semaphore_signal(barrier, inc=1, device_id={"scheme": lax.rem(g + i, groups)})

    def greet_scen(i):
        pl.semaphore_signal(barrier, inc=1, device_id={"scen": lax.rem(c + i, parts)})

    each(1, groups, greet)
    each(1, parts, greet_scen)

    def to_scheme(src, dst, ss, rs, i):
        return pltpu.make_async_remote_copy(
            src_ref=src, dst_ref=dst, send_sem=ss.at[i], recv_sem=rs.at[i],
            device_id={"scheme": lax.rem(g + i, groups)})

    def comp_copy(i):
        return to_scheme(comp_send.at[block(i, pad), mine], comp_recv.at[block(i, pad), mine], comp_ss, comp_rs, i)

    def strip_copy(i):
        return pltpu.make_async_remote_copy(
            src_ref=comp_recv.at[pad:, mine], dst_ref=comp_recv.at[pad:, mine],
            send_sem=strip_ss.at[i], recv_sem=strip_rs.at[i],
            device_id={"scen": lax.rem(c + i, parts)})

    def strip_arrival(i):
        strip = comp_recv.at[pad:, block(lax.rem(c - i + parts, parts), lanes)]
        return pltpu.make_async_remote_copy(
            src_ref=strip, dst_ref=strip,
            send_sem=strip_ss.at[i], recv_sem=strip_rs.at[i],
            device_id={"scen": lax.rem(c + i, parts)})

    def flag_copy(i):
        return to_scheme(flag_send.at[block(i, pad)], flag_recv.at[block(i, pad)], flag_ss, flag_rs, i)

    def held_copy(i):
        return to_scheme(held_send.at[i], held_recv.at[i], held_ss, held_rs, i)

    def claim_copy(i):
        return to_scheme(claim_send, claim_recv.at[i], claim_ss, claim_rs, i)

    def base_copy(i):
        return pltpu.make_async_remote_copy(
            src_ref=base_send, dst_ref=base_recv.at[i], send_sem=base_ss.at[i], recv_sem=base_rs.at[i],
            device_id={"scen": lax.rem(c + i, parts)})

    in_owner.wait()
    rel = lax.rem(owner_v[...] - g + groups, groups)
    hits = (rel == lax.broadcasted_iota(jnp.int32, (groups, rows), 0)).astype(jnp.float32)
    upper = (lax.broadcasted_iota(jnp.int32, (rows, rows), 0)
             < lax.broadcasted_iota(jnp.int32, (rows, rows), 1)).astype(jnp.bfloat16)
    hits_b = hits.astype(jnp.bfloat16)
    earlier = jnp.dot(hits_b, upper, preferred_element_type=jnp.float32)
    rank = jnp.sum(earlier * hits, axis=0, keepdims=True).astype(jnp.int32)
    slot = rel * pad + rank
    pick = (slot == lax.broadcasted_iota(jnp.int32, (groups * pad, rows), 0)).astype(jnp.bfloat16)

    in_cash.wait()
    cash_t = cash_v[...]
    comp_t = jnp.minimum(0.9 * cash_t.astype(jnp.float32), COMP_LIMIT).astype(jnp.bfloat16)
    comp_rows = lax.dot_general(pick, comp_t, NT, preferred_element_type=jnp.float32).astype(jnp.bfloat16)
    comp_send[:, :width] = comp_rows
    if comp_send.shape[1] > width:
        comp_send[:, width:] = jnp.zeros((comp_send.shape[0], comp_send.shape[1] - width), jnp.bfloat16)

    comp_recv[0:pad, :width] = comp_rows[0:pad]

    in_flags.wait()
    flags = [flags_v[:, y, :].astype(jnp.float32) for y in range(years)]
    for y in range(years):
        flag_send[:, y * n:(y + 1) * n] = jnp.dot(
            pick, flags[y].astype(jnp.bfloat16), preferred_element_type=jnp.float32).astype(jnp.bfloat16)
    pl.semaphore_wait(barrier, groups + parts - 2)
    each(1, groups, lambda i: comp_copy(i).start())
    each(1, groups, lambda i: flag_copy(i).start())

    in_returns.wait()
    in_alloc.wait()
    in_share.wait()
    in_assets0.wait()
    eye = (lax.broadcasted_iota(jnp.int32, (rows, rows), 0)
           == lax.broadcasted_iota(jnp.int32, (rows, rows), 1))
    class_id = lax.broadcasted_iota(jnp.int32, (classes, rows), 0)
    exposure_t = jnp.zeros((classes, rows), jnp.float32)
    for j in range(alloc_v.shape[0]):
        exposure_t = exposure_t + jnp.where(alloc_v[j:j + 1, :] == class_id, share_v[j:j + 1, :], 0.0)
    assets = jnp.sum(jnp.where(eye, assets0_v[...], 0.0), axis=1, keepdims=True)
    held = []
    for y in range(years):
        growth = lax.dot_general(exposure_t, returns_v[y], TN, precision=HIGHEST,
                                 preferred_element_type=jnp.float32)
        assets = assets * jnp.exp(growth)
        held.append(assets)
        held_send[:, y, :] = sum(jnp.dot(hits_b, piece, preferred_element_type=jnp.float32)
                                 for piece in pieces(flags[y] * assets))
    each(1, groups, lambda i: held_copy(i).start())


    in_rates.wait()
    in_infl.wait()
    neg_terms = -(lax.broadcasted_iota(jnp.int32, (hor, n), 0) + 1).astype(jnp.float32)
    short = jnp.zeros((rows, n), jnp.float32)
    for y in range(years):
        rate = rates_v[:, y, :]
        infl = infl_v[:, y, :]
        for k, index in enumerate(TRANCHE_INDEX):
            disc_v[y, k * hor:(k + 1) * hor, :] = jnp.exp(neg_terms * (rate - index * infl))
        liab = lax.dot_general(cash_t, disc_v[y].astype(jnp.bfloat16), TN,
                               preferred_element_type=jnp.float32)
        short = short + (jnp.maximum(liab - held[y], 0.0) + 0.05 * liab)
    each(1, groups, lambda i: comp_copy(i).wait_recv())
    each(1, parts, lambda i: strip_copy(i).start())
    base_send[...] = jnp.sum(jnp.where(eye, jnp.sum(short, axis=1, keepdims=True), 0.0), axis=0, keepdims=True)
    each(1, parts, lambda i: base_copy(i).start())

    in_basis.wait()
    basis = basis_v[0].astype(jnp.float32)
    factors = [(basis * disc_v[y].astype(jnp.bfloat16).astype(jnp.float32)).astype(jnp.bfloat16)
               for y in range(years)]
    each(1, parts, lambda i: strip_arrival(i).wait_recv())
    for y in range(years):
        value_v[:, y * n:(y + 1) * n] = jnp.dot(comp_recv[:, :width], factors[y],
                                                preferred_element_type=jnp.float32)
    value_v[0:pad] = flag_send[0:pad].astype(jnp.float32) * value_v[0:pad]

    each(1, parts, lambda i: base_copy(i).wait_recv())
    base = base_send[...]
    for i in range(1, parts):
        base = base + base_recv[i]
    base = base / (n * parts * years)
    base_ref[...] = base
    claim_send[years:years + 1, :] = jnp.broadcast_to(jnp.sum(base, axis=1, keepdims=True), (1, n))
    each(1, groups, lambda i: held_copy(i).wait_recv())
    held_recv[0] = held_send[0]
    held_sum = [jnp.sum(held_recv[:, y, :], axis=0, keepdims=True) for y in range(years)]

    def add_book(i):
        flag_copy(i).wait_recv()
        at = block(i, pad)
        value_v[0:pad] = value_v[0:pad] + flag_recv[at].astype(jnp.float32) * value_v[at]

    each(1, groups, add_book)
    summed = jnp.sum(value_v[0:pad], axis=0, keepdims=True)
    book = [summed[:, y * n:(y + 1) * n] for y in range(years)]
    for y in range(years):
        book[y] = book[y] - held_sum[y]
        claim_send[y:y + 1, :] = book[y]
        book_ref[0, y:y + 1, :] = book[y]

    each(1, groups, lambda i: claim_copy(i).start())
    claim_recv[0] = claim_send[...]
    each(1, groups, lambda i: comp_copy(i).wait_send())
    each(1, parts, lambda i: strip_copy(i).wait_send())
    each(1, groups, lambda i: flag_copy(i).wait_send())
    each(1, groups, lambda i: held_copy(i).wait_send())
    each(1, parts, lambda i: base_copy(i).wait_send())
    each(1, groups, lambda i: claim_copy(i).wait_recv())
    total = jnp.sum(claim_recv[...], axis=0)
    for y in range(years):
        coef_ref[y:y + 1, :] = (total[y:y + 1, :] / groups) / (total[years:years + 1, :] / (rows * groups))

    each(1, groups, lambda i: claim_copy(i).wait_send())


def spread(book_in, coef_ref, base_ref, book_ref, levy_ref):
    rows, years, n = levy_ref.shape
    eye = (lax.broadcasted_iota(jnp.int32, (rows, rows), 0)
           == lax.broadcasted_iota(jnp.int32, (rows, rows), 1))
    base = jnp.sum(jnp.where(eye, base_ref[...], 0.0), axis=1, keepdims=True)
    book_ref[...] = book_in[...]
    for y in range(years):
        levy_ref[:, y, :] = coef_ref[y:y + 1, :] * base


def shards(cashflow, assets0, alloc, share, owner, flags, rates, inflation, returns, basis):
    rows, width = cashflow.shape
    years, hor, n = rates.shape
    classes = returns.shape[1]
    hold = alloc.shape[1]
    groups = lax.axis_size("scheme")
    parts = lax.axis_size("scen")
    cap = max(2, (2 * rows + groups - 1) // groups)
    pad = -(-cap // 16) * 16
    lanes = -(-width // (128 * parts)) * 128
    f32, bf16, i32 = jnp.float32, jnp.bfloat16, jnp.int32
    dma = pltpu.SemaphoreType.DMA
    book, coef, base = pl.pallas_call(
        functools.partial(kernel, groups, pad, parts),
        out_shape=(jax.ShapeDtypeStruct((1, years, n), f32),
                   jax.ShapeDtypeStruct((years, n), f32),
                   jax.ShapeDtypeStruct((1, rows), f32)),
        in_specs=[pl.BlockSpec(memory_space=pltpu.HBM)] * 10,
        out_specs=(pl.BlockSpec(memory_space=pltpu.VMEM),) * 3,
        scratch_shapes=[
            pltpu.VMEM((1, rows), i32),
            pltpu.VMEM((width, rows), bf16),
            pltpu.VMEM((rows, years, n), i32),
            pltpu.VMEM((hor, years, n), f32),
            pltpu.VMEM((hor, years, n), f32),
            pltpu.VMEM((years, classes, n), f32),
            pltpu.VMEM((hold, rows), i32),
            pltpu.VMEM((hold, rows), f32),
            pltpu.VMEM((1, rows), f32),
            pltpu.VMEM((1, width, n), bf16),
            pltpu.VMEM((groups * pad, parts * lanes), bf16),
            pltpu.VMEM((groups * pad, parts * lanes), bf16),
            pltpu.VMEM((groups * pad, years * n), bf16),
            pltpu.VMEM((groups * pad, years * n), bf16),
            pltpu.VMEM((years, width, n), f32),
            pltpu.VMEM((groups, years, n), f32),
            pltpu.VMEM((groups, years, n), f32),
            pltpu.VMEM((1, rows), f32),
            pltpu.VMEM((parts, 1, rows), f32),
            pltpu.VMEM((years + 1, n), f32),
            pltpu.VMEM((groups, years + 1, n), f32),
            pltpu.VMEM((groups * pad, years * n), f32),
            dma((parts,)), dma((parts,)),
            dma((10,)),
            dma((groups,)), dma((groups,)),
            dma((groups,)), dma((groups,)),
            dma((groups,)), dma((groups,)),
            dma((parts,)), dma((parts,)),
            dma((groups,)), dma((groups,)),
        ],
        compiler_params=pltpu.CompilerParams(
            collective_id=0, has_side_effects=True, vmem_limit_bytes=40 * 2**20),
        name="fund",
    )(*(pltpu.with_memory_space_constraint(x, pltpu.HBM) for x in (
        owner.T, cashflow.T, flags, rates.transpose(1, 0, 2), inflation.transpose(1, 0, 2), returns,
        alloc.T, share.T, assets0.reshape(1, rows), basis)))
    book, levy = pl.pallas_call(
        spread,
        out_shape=(jax.ShapeDtypeStruct((1, years, n), f32), jax.ShapeDtypeStruct((rows, years, n), f32)),
        in_specs=[pl.BlockSpec(memory_space=pltpu.VMEM)] * 3,
        out_specs=(pl.BlockSpec(memory_space=pltpu.VMEM),) * 2,
        compiler_params=pltpu.CompilerParams(vmem_limit_bytes=4 * 2**20),
        name="spread",
    )(book, coef, base)
    return book, levy


def solution(mesh):
    placed = (
        P("scheme", None),
        P("scheme"),
        P("scheme", None),
        P("scheme", None),
        P("scheme", None),
        P("scheme", None, "scen"),
        P(None, None, "scen"),
        P(None, None, "scen"),
        P(None, None, "scen"),
        P("scheme", None, "scen"),
    )
    return jax.shard_map(
        shards,
        mesh=mesh,
        in_specs=placed,
        out_specs=(P("scheme", None, "scen"), P("scheme", None, "scen")),
        check_vma=False,
    )
```

```python
import functools

import jax
import jax.numpy as jnp
from jax import lax
from jax.experimental import pallas as pl
from jax.experimental.pallas import tpu as pltpu
from jax.sharding import PartitionSpec as P

TRANCHE_INDEX = (0.0, 0.5, 1.0, 0.75)
COMP_LIMIT = 0.004
HIGHEST = lax.Precision.HIGHEST
NT = (((1,), (1,)), ((), ()))
TN = (((0,), (0,)), ((), ()))


def each(low, high, body):
    if high - low <= 16:
        for i in range(low, high):
            body(i)
    else:
        lax.fori_loop(low, high, lambda i, c: (body(i), c)[1], 0)


def pieces(x):
    high = x.astype(jnp.bfloat16)
    rest = x - high.astype(jnp.float32)
    middle = rest.astype(jnp.bfloat16)
    low = (rest - middle.astype(jnp.float32)).astype(jnp.bfloat16)
    return high, middle, low


def block(i, size):
    start = i * size
    return pl.ds(start if isinstance(start, int) else pl.multiple_of(start, size), size)


def kernel(groups, pad, parts,
           owner_h, cash_h, flags_h, rates_h, infl_h, returns_h, alloc_h, share_h, assets0_h, basis_h,
           book_ref, coef_ref, base_ref,
           owner_v, cash_v, flags_v, rates_v, infl_v, returns_v, alloc_v, share_v, assets0_v, basis_v,
           comp_send, comp_recv, flag_send, flag_recv, disc_v, held_send, held_recv,
           base_send, base_recv, claim_send, claim_recv,
           value_v, strip_ss, strip_rs,
           local_sem, comp_ss, comp_rs, flag_ss, flag_rs, held_ss, held_rs, base_ss, base_rs, claim_ss, claim_rs):
    g = lax.axis_index("scheme")
    c = lax.axis_index("scen")
    rows = owner_v.shape[1]
    years = rates_v.shape[1]
    hor = rates_v.shape[0]
    n = rates_v.shape[2]
    classes = returns_v.shape[1]
    width = cash_v.shape[0]
    lanes = comp_send.shape[1] // parts
    mine = block(c, lanes)

    def local(k, src, dst):
        copy = pltpu.make_async_copy(src, dst, local_sem.at[k])
        copy.start()
        return copy

    in_owner = local(0, owner_h, owner_v)
    in_cash = local(2, cash_h, cash_v)
    in_flags = local(1, flags_h, flags_v)
    in_rates = local(3, rates_h, rates_v)
    in_infl = local(4, infl_h, infl_v)
    in_returns = local(5, returns_h, returns_v)
    in_alloc = local(6, alloc_h, alloc_v)
    in_share = local(7, share_h, share_v)
    in_assets0 = local(8, assets0_h, assets0_v)
    in_basis = local(9, basis_h, basis_v)

    barrier = pltpu.get_barrier_semaphore()

    def greet(i):
        pl.semaphore_signal(barrier, inc=1, device_id={"scheme": lax.rem(g + i, groups)})

    def greet_scen(i):
        pl.semaphore_signal(barrier, inc=1, device_id={"scen": lax.rem(c + i, parts)})

    each(1, groups, greet)
    each(1, parts, greet_scen)

    def to_scheme(src, dst, ss, rs, i):
        return pltpu.make_async_remote_copy(
            src_ref=src, dst_ref=dst, send_sem=ss.at[i], recv_sem=rs.at[i],
            device_id={"scheme": lax.rem(g + i, groups)})

    def comp_copy(i):
        return to_scheme(comp_send.at[block(i, pad), mine], comp_recv.at[block(i, pad), mine], comp_ss, comp_rs, i)

    def strip_copy(i):
        return pltpu.make_async_remote_copy(
            src_ref=comp_recv.at[pad:, mine], dst_ref=comp_recv.at[pad:, mine],
            send_sem=strip_ss.at[i], recv_sem=strip_rs.at[i],
            device_id={"scen": lax.rem(c + i, parts)})

    def strip_arrival(i):
        strip = comp_recv.at[pad:, block(lax.rem(c - i + parts, parts), lanes)]
        return pltpu.make_async_remote_copy(
            src_ref=strip, dst_ref=strip,
            send_sem=strip_ss.at[i], recv_sem=strip_rs.at[i],
            device_id={"scen": lax.rem(c + i, parts)})

    def flag_copy(i):
        return to_scheme(flag_send.at[block(i, pad)], flag_recv.at[block(i, pad)], flag_ss, flag_rs, i)

    def held_copy(i):
        return to_scheme(held_send.at[i], held_recv.at[i], held_ss, held_rs, i)

    def claim_copy(i):
        return to_scheme(claim_send, claim_recv.at[i], claim_ss, claim_rs, i)

    def base_copy(i):
        return pltpu.make_async_remote_copy(
            src_ref=base_send, dst_ref=base_recv.at[i], send_sem=base_ss.at[i], recv_sem=base_rs.at[i],
            device_id={"scen": lax.rem(c + i, parts)})

    in_owner.wait()
    rel = lax.rem(owner_v[...] - g + groups, groups)
    hits = (rel == lax.broadcasted_iota(jnp.int32, (groups, rows), 0)).astype(jnp.float32)
    upper = (lax.broadcasted_iota(jnp.int32, (rows, rows), 0)
             < lax.broadcasted_iota(jnp.int32, (rows, rows), 1)).astype(jnp.bfloat16)
    hits_b = hits.astype(jnp.bfloat16)
    earlier = jnp.dot(hits_b, upper, preferred_element_type=jnp.float32)
    rank = jnp.sum(earlier * hits, axis=0, keepdims=True).astype(jnp.int32)
    slot = rel * pad + rank
    pick = (slot == lax.broadcasted_iota(jnp.int32, (groups * pad, rows), 0)).astype(jnp.bfloat16)

    in_cash.wait()
    cash_t = cash_v[...]
    comp_t = jnp.minimum(0.9 * cash_t.astype(jnp.float32), COMP_LIMIT).astype(jnp.bfloat16)
    comp_rows = lax.dot_general(pick, comp_t, NT, preferred_element_type=jnp.float32).astype(jnp.bfloat16)
    comp_send[:, :width] = comp_rows
    if comp_send.shape[1] > width:
        comp_send[:, width:] = jnp.zeros((comp_send.shape[0], comp_send.shape[1] - width), jnp.bfloat16)

    comp_recv[0:pad, :width] = comp_rows[0:pad]

    in_flags.wait()
    flags = [flags_v[:, y, :].astype(jnp.float32) for y in range(years)]
    for y in range(years):
        flag_send[:, y * n:(y + 1) * n] = jnp.dot(
            pick, flags[y].astype(jnp.bfloat16), preferred_element_type=jnp.float32).astype(jnp.bfloat16)
    pl.semaphore_wait(barrier, groups + parts - 2)
    each(1, groups, lambda i: comp_copy(i).start())
    each(1, groups, lambda i: flag_copy(i).start())

    in_returns.wait()
    in_alloc.wait()
    in_share.wait()
    in_assets0.wait()
    eye = (lax.broadcasted_iota(jnp.int32, (rows, rows), 0)
           == lax.broadcasted_iota(jnp.int32, (rows, rows), 1))
    class_id = lax.broadcasted_iota(jnp.int32, (classes, rows), 0)
    exposure_t = jnp.zeros((classes, rows), jnp.float32)
    for j in range(alloc_v.shape[0]):
        exposure_t = exposure_t + jnp.where(alloc_v[j:j + 1, :] == class_id, share_v[j:j + 1, :], 0.0)
    assets = jnp.sum(jnp.where(eye, assets0_v[...], 0.0), axis=1, keepdims=True)
    held = []
    for y in range(years):
        growth = lax.dot_general(exposure_t, returns_v[y], TN, precision=HIGHEST,
                                 preferred_element_type=jnp.float32)
        assets = assets * jnp.exp(growth)
        held.append(assets)
        held_send[:, y, :] = sum(jnp.dot(hits_b, piece, preferred_element_type=jnp.float32)
                                 for piece in pieces(flags[y] * assets))
    each(1, groups, lambda i: held_copy(i).start())


    each(1, groups, lambda i: comp_copy(i).wait_recv())
    each(1, parts, lambda i: strip_copy(i).start())

    in_rates.wait()
    in_infl.wait()
    neg_terms = -(lax.broadcasted_iota(jnp.int32, (hor, n), 0) + 1).astype(jnp.float32)
    short = jnp.zeros((rows, n), jnp.float32)
    cash = lax.dot_general(eye.astype(jnp.bfloat16), cash_t, NT,
                           preferred_element_type=jnp.float32).astype(jnp.bfloat16)
    discs = []
    for y in range(years):
        rate = rates_v[:, y, :]
        infl = infl_v[:, y, :]
        for k, index in enumerate(TRANCHE_INDEX):
            disc_v[y, k * hor:(k + 1) * hor, :] = jnp.exp(neg_terms * (rate - index * infl))
        disc = disc_v[y].astype(jnp.bfloat16)
        liab = jnp.dot(cash, disc, preferred_element_type=jnp.float32)
        discs.append(disc)
        short = short + (jnp.maximum(liab - held[y], 0.0) + 0.05 * liab)
    base_send[...] = jnp.sum(jnp.where(eye, jnp.sum(short, axis=1, keepdims=True), 0.0), axis=0, keepdims=True)
    each(1, parts, lambda i: base_copy(i).start())

    in_basis.wait()
    basis = basis_v[0].astype(jnp.float32)
    factors = [(basis * discs[y].astype(jnp.float32)).astype(jnp.bfloat16)
               for y in range(years)]
    each(1, parts, lambda i: strip_arrival(i).wait_recv())
    for y in range(years):
        value_v[:, y * n:(y + 1) * n] = jnp.dot(comp_recv[:, :width], factors[y],
                                                preferred_element_type=jnp.float32)
    value_v[0:pad] = flag_send[0:pad].astype(jnp.float32) * value_v[0:pad]

    each(1, parts, lambda i: base_copy(i).wait_recv())
    base = base_send[...]
    for i in range(1, parts):
        base = base + base_recv[i]
    base = base / (n * parts * years)
    base_ref[...] = base
    claim_send[years:years + 1, :] = jnp.broadcast_to(jnp.sum(base, axis=1, keepdims=True), (1, n))
    each(1, groups, lambda i: held_copy(i).wait_recv())
    held_recv[0] = held_send[0]
    held_sum = [jnp.sum(held_recv[:, y, :], axis=0, keepdims=True) for y in range(years)]

    def add_book(i):
        flag_copy(i).wait_recv()
        at = block(i, pad)
        value_v[0:pad] = value_v[0:pad] + flag_recv[at].astype(jnp.float32) * value_v[at]

    each(1, groups, add_book)
    summed = jnp.sum(value_v[0:pad], axis=0, keepdims=True)
    book = [summed[:, y * n:(y + 1) * n] for y in range(years)]
    for y in range(years):
        book[y] = book[y] - held_sum[y]
        claim_send[y:y + 1, :] = book[y]
        book_ref[0, y:y + 1, :] = book[y]

    each(1, groups, lambda i: claim_copy(i).start())
    claim_recv[0] = claim_send[...]
    each(1, groups, lambda i: comp_copy(i).wait_send())
    each(1, parts, lambda i: strip_copy(i).wait_send())
    each(1, groups, lambda i: flag_copy(i).wait_send())
    each(1, groups, lambda i: held_copy(i).wait_send())
    each(1, parts, lambda i: base_copy(i).wait_send())
    each(1, groups, lambda i: claim_copy(i).wait_recv())
    total = jnp.sum(claim_recv[...], axis=0)
    for y in range(years):
        coef_ref[y:y + 1, :] = (total[y:y + 1, :] / groups) / (total[years:years + 1, :] / (rows * groups))

    each(1, groups, lambda i: claim_copy(i).wait_send())


def spread(book_in, coef_ref, base_ref, book_ref, levy_ref):
    rows, years, n = levy_ref.shape
    eye = (lax.broadcasted_iota(jnp.int32, (rows, rows), 0)
           == lax.broadcasted_iota(jnp.int32, (rows, rows), 1))
    base = jnp.sum(jnp.where(eye, base_ref[...], 0.0), axis=1, keepdims=True)
    book_ref[...] = book_in[...]
    for y in range(years):
        levy_ref[:, y, :] = coef_ref[y:y + 1, :] * base


def shards(cashflow, assets0, alloc, share, owner, flags, rates, inflation, returns, basis):
    rows, width = cashflow.shape
    years, hor, n = rates.shape
    classes = returns.shape[1]
    hold = alloc.shape[1]
    groups = lax.axis_size("scheme")
    parts = lax.axis_size("scen")
    cap = max(2, (2 * rows + groups - 1) // groups)
    pad = -(-cap // 16) * 16
    lanes = -(-width // (128 * parts)) * 128
    f32, bf16, i32 = jnp.float32, jnp.bfloat16, jnp.int32
    dma = pltpu.SemaphoreType.DMA
    book, coef, base = pl.pallas_call(
        functools.partial(kernel, groups, pad, parts),
        out_shape=(jax.ShapeDtypeStruct((1, years, n), f32),
                   jax.ShapeDtypeStruct((years, n), f32),
                   jax.ShapeDtypeStruct((1, rows), f32)),
        in_specs=[pl.BlockSpec(memory_space=pltpu.HBM)] * 10,
        out_specs=(pl.BlockSpec(memory_space=pltpu.VMEM),) * 3,
        scratch_shapes=[
            pltpu.VMEM((1, rows), i32),
            pltpu.VMEM((width, rows), bf16),
            pltpu.VMEM((rows, years, n), i32),
            pltpu.VMEM((hor, years, n), f32),
            pltpu.VMEM((hor, years, n), f32),
            pltpu.VMEM((years, classes, n), f32),
            pltpu.VMEM((hold, rows), i32),
            pltpu.VMEM((hold, rows), f32),
            pltpu.VMEM((1, rows), f32),
            pltpu.VMEM((1, width, n), bf16),
            pltpu.VMEM((groups * pad, parts * lanes), bf16),
            pltpu.VMEM((groups * pad, parts * lanes), bf16),
            pltpu.VMEM((groups * pad, years * n), bf16),
            pltpu.VMEM((groups * pad, years * n), bf16),
            pltpu.VMEM((years, width, n), f32),
            pltpu.VMEM((groups, years, n), f32),
            pltpu.VMEM((groups, years, n), f32),
            pltpu.VMEM((1, rows), f32),
            pltpu.VMEM((parts, 1, rows), f32),
            pltpu.VMEM((years + 1, n), f32),
            pltpu.VMEM((groups, years + 1, n), f32),
            pltpu.VMEM((groups * pad, years * n), f32),
            dma((parts,)), dma((parts,)),
            dma((10,)),
            dma((groups,)), dma((groups,)),
            dma((groups,)), dma((groups,)),
            dma((groups,)), dma((groups,)),
            dma((parts,)), dma((parts,)),
            dma((groups,)), dma((groups,)),
        ],
        compiler_params=pltpu.CompilerParams(
            collective_id=0, has_side_effects=True, vmem_limit_bytes=40 * 2**20),
        name="fund",
    )(*(pltpu.with_memory_space_constraint(x, pltpu.HBM) for x in (
        owner.T, cashflow.T, flags, rates.transpose(1, 0, 2), inflation.transpose(1, 0, 2), returns,
        alloc.T, share.T, assets0.reshape(1, rows), basis)))
    book, levy = pl.pallas_call(
        spread,
        out_shape=(jax.ShapeDtypeStruct((1, years, n), f32), jax.ShapeDtypeStruct((rows, years, n), f32)),
        in_specs=[pl.BlockSpec(memory_space=pltpu.VMEM)] * 3,
        out_specs=(pl.BlockSpec(memory_space=pltpu.VMEM),) * 2,
        compiler_params=pltpu.CompilerParams(vmem_limit_bytes=4 * 2**20),
        name="spread",
    )(book, coef, base)
    return book, levy


def solution(mesh):
    placed = (
        P("scheme", None),
        P("scheme"),
        P("scheme", None),
        P("scheme", None),
        P("scheme", None),
        P("scheme", None, "scen"),
        P(None, None, "scen"),
        P(None, None, "scen"),
        P(None, None, "scen"),
        P("scheme", None, "scen"),
    )
    return jax.shard_map(
        shards,
        mesh=mesh,
        in_specs=placed,
        out_specs=(P("scheme", None, "scen"), P("scheme", None, "scen")),
        check_vma=False,
    )
```
